128 devices in a mesh: row: 8 (over y, core), col: 16 (over z, x).
Axes of the slice: x: 4, y: 4, z: 4, core: 2. Of those that a mesh axis runs over, the one named last changes fastest.
Arguments:
- chol_window: bfloat16 [48, 48, 1536], P(None, None, ('row', 'col')), may hold values from -0.3125 to 0.3125
- chol_pairs: bfloat16 [512, 512, 1536], P('row', 'col'), may hold values from -0.3125 to 0.3125
- amplitudes: bfloat16 [48, 512, 1024], P(None, 'col', 'row'), may hold values from -6 to 6
- eps_window: float32 [48], P('col'), may hold values from 0.5 to 2
- eps_virtual: float32 [512], P('row'), may hold values from 0.5 to 2
- eps_occupied: float32 [1024], replicated, may hold values from 0.5 to 2
- dress_first: bfloat16 [1024, 1024], replicated, may hold values from -0.1875 to 0.1875
- dress_second: bfloat16 [1024, 1024], replicated, may hold values from -0.1875 to 0.1875
Outputs:
- resid: bfloat16 [48, 512, 1024], P('col', None, 'row')
The draws below stay inside these ranges and needn't reach their ends.
All inputs are finite; a program needn't handle non-finite values.
Results may differ from the reference program's by a relative error of at most 0.0061.
Values may be sent and summed in bfloat16 or wider, within the bound.
No kernel may reach another device: no remote copies, remote signals or barrier semaphores. Data moves between devices by JAX's collectives and lax.ppermute only.
A program may use at most 192 MiB of HBM per device.

```python
import math
import jax
import jax.numpy as jnp
from jax import lax

VIRT = 512
NAUX = 1536
OCC = 1024
VW = 48


def shard_levels(stream_key, shape, pieces, least, largest):
    loudness = 1.0
    for dim, blocks in pieces:
        heights = jax.random.uniform(jax.random.fold_in(jax.random.fold_in(stream_key, 6), dim), (blocks,), jnp.float32, least / len(pieces), largest / len(pieces))
        loudness = loudness * jnp.repeat(jnp.exp(heights), shape[dim] // blocks).reshape((-1,) + (1,) * (len(shape) - 1 - dim))
    return loudness


def normal_values(rng, shape, scale, limit, split=(), dtype=jnp.bfloat16):
    result = jax.random.normal(rng, shape, jnp.float32) * scale
    if len(split) > 0:
        result = shard_levels(rng, shape, split, -0.22, 0.18) * result
    return jnp.clip(result, min=-limit, max=limit).astype(dtype)


def setup_inputs(seed: int = 0) -> dict:
    arg_keys = jax.random.split(jax.random.key(seed), 9)
    return {
        "chol_window": normal_values(arg_keys[0], (VW, VW, NAUX), ((3.0 / (VW * VIRT * NAUX) ** 0.5) ** 0.5), 0.3125, ((2, 128),)),
        "chol_pairs": normal_values(arg_keys[1], (VIRT, VIRT, NAUX), ((3.0 / (VW * VIRT * NAUX) ** 0.5) ** 0.5), 0.3125, ((0, 8), (1, 16))),
        "amplitudes": normal_values(arg_keys[2], (VW, VIRT, OCC), 1.0, 6.0, ((1, 16), (2, 8))),
        "eps_window": jnp.clip(jnp.exp(math.log(2.0) - 1.3862944 * jax.random.uniform(arg_keys[3], (VW,), jnp.float32) ** shard_levels(arg_keys[3], (VW,), ((0, 16),), -0.2, 0.2)), 0.5, 2.0),
        "eps_virtual": jnp.clip(jnp.exp(math.log(2.0) - 1.3862944 * jax.random.uniform(arg_keys[4], (VIRT,), jnp.float32) ** shard_levels(arg_keys[4], (VIRT,), ((0, 8),), -0.2, 0.2)), 0.5, 2.0),
        "eps_occupied": jnp.clip(jnp.exp(jax.random.uniform(arg_keys[5], (OCC,), jnp.float32, math.log(0.5), math.log(2.0))), 0.5, 2.0),
        "dress_first": normal_values(arg_keys[6], (OCC, OCC), OCC ** -0.5, 0.1875),
        "dress_second": normal_values(arg_keys[7], (OCC, OCC), OCC ** -0.5, 0.1875),
    }


def reference(chol_window, chol_pairs, amplitudes, eps_window, eps_virtual, eps_occupied, dress_first, dress_second):
    window_f32 = chol_window.astype(jnp.float32)
    pairs_f32 = chol_pairs.astype(jnp.float32)
    amp_f32 = amplitudes.astype(jnp.float32)

    def per_virtual(aux_row):
        tile = jnp.einsum("cq,bdq->bcd", aux_row, pairs_f32).astype(jnp.bfloat16)
        tile = lax.optimization_barrier(tile).astype(jnp.float32)
        return jnp.einsum("bcd,cdo->bo", tile, amp_f32)

    ladder = lax.map(per_virtual, window_f32)
    denominator = eps_window[:, None, None] + eps_virtual[None, :, None] + eps_occupied[None, None, :]
    scaled = (ladder / denominator).astype(jnp.bfloat16)
    flattened = scaled.reshape(VW * VIRT, OCC)
    first_mix = jnp.dot(flattened, dress_first, preferred_element_type=jnp.float32).astype(jnp.bfloat16)
    mixed = flattened.astype(jnp.float32) + jnp.dot(first_mix, dress_second, preferred_element_type=jnp.float32)
    return mixed.astype(jnp.bfloat16).reshape(VW, VIRT, OCC)
```

```python
import functools

import jax
import jax.numpy as jnp
from jax import lax
from jax.experimental import pallas as pl
from jax.experimental.pallas import tpu as pltpu
from jax.sharding import PartitionSpec as P

AXES = ("row", "col")
BF = jnp.bfloat16
F32 = jnp.float32
NT = (((1,), (1,)), ((), ()))


def linear(y, c, z, x):
    return (((y % 4) * 2 + c % 2) * 4 + z % 4) * 4 + x % 4


def pairs(move):
    return [
        (linear(y, c, z, x), linear(*move(y, c, z, x)))
        for y in range(4)
        for c in range(2)
        for z in range(4)
        for x in range(4)
    ]


def send(value, move):
    return lax.ppermute(value, AXES, pairs(move))


def shift_y(s):
    return lambda y, c, z, x: (y + s, c, z, x)


def swap_core(y, c, z, x):
    return (y, 1 - c, z, x)


def shift_first(s):
    return lambda y, c, z, x: (y, c, z + s * (1 - c), x + s * c)


def shift_second(s):
    return lambda y, c, z, x: (y, c, z + s * c, x + s * (1 - c))


def prepare_pairs(chol_pairs, order):
    block_b, block_d, aux = chol_pairs.shape

    def kernel(order_ref, in_ref, out_ref, columns):
        @pl.when((pl.program_id(0) == 0) & (pl.program_id(1) == 0))
        def _():
            q = lax.broadcasted_iota(jnp.int32, (aux, aux), 0)
            columns[...] = jnp.where(q == order_ref[...], 1.0, 0.0).astype(BF)

        target = lax.broadcasted_iota(jnp.int32, (256, 256), 0)
        source = lax.broadcasted_iota(jnp.int32, (256, 256), 1)
        rows = jnp.where((target % 16) * 16 + target // 16 == source, 1.0, 0.0).astype(BF)
        block = in_ref[...].reshape(256, aux)
        block = jnp.dot(rows, block, preferred_element_type=F32).astype(BF)
        block = jnp.dot(block, columns[...], preferred_element_type=F32).astype(BF)
        out_ref[...] = block.reshape(16, 16, aux)

    return pl.pallas_call(
        kernel,
        grid=(block_b // 16, block_d // 16),
        in_specs=[
            pl.BlockSpec((1, aux), lambda i, j: (0, 0)),
            pl.BlockSpec((16, 16, aux), lambda i, j: (i, j, 0)),
        ],
        out_specs=pl.BlockSpec((16, 16, aux), lambda i, j: (j, i, 0)),
        out_shape=jax.ShapeDtypeStruct((block_d, block_b, aux), BF),
        scratch_shapes=[pltpu.VMEM((aux, aux), BF)],
        name="prepare_pairs",
    )(order, chol_pairs)


def turn_window(mine, theirs):
    lanes = mine[0].shape[2]
    step = 384
    count = lanes // step
    aux = 4 * 4 * 96

    def kernel(*refs):
        mine_refs, their_refs, out_ref = refs[:4], refs[4:8], refs[8]
        eye = (
            lax.broadcasted_iota(jnp.int32, (128, 128), 0)
            == lax.broadcasted_iota(jnp.int32, (128, 128), 1)
        )
        eye = jnp.where(eye, 1.0, 0.0).astype(BF)

        def put(value, slot):
            for n in range(step // 128):
                turned = lax.dot_general(
                    eye, value[:, n * 128 : (n + 1) * 128], NT, preferred_element_type=F32
                )
                out_ref[n * 128 : (n + 1) * 128, slot * 384 : (slot + 1) * 384] = turned.astype(BF)

        @pl.when(pl.program_id(0) == 0)
        def _():
            for s in range(4):
                put(mine_refs[s][...].reshape(384, step), s)

        @pl.when(pl.program_id(0) == 1)
        def _():
            for m in range(4):
                put(jnp.concatenate([their_refs[s][m] for s in range(4)], axis=0), m)

    mine_spec = pl.BlockSpec((4, 96, step), lambda h, j: (0, 0, j * (1 - h) + (count - 1) * h))
    their_spec = pl.BlockSpec((4, 96, step), lambda h, j: (0, 0, j * h))
    return pl.pallas_call(
        kernel,
        grid=(2, count),
        in_specs=[mine_spec] * 4 + [their_spec] * 4,
        out_specs=pl.BlockSpec((step, aux), lambda h, j: (h * count + j, 0)),
        out_shape=jax.ShapeDtypeStruct((2 * lanes, aux), BF),
        name="turn_window",
    )(*mine, *theirs)


def ladder_block(index, window, pairs_block, amp_mine, amp_theirs):
    rows_c, aux = window.shape[1], window.shape[2]
    block_d, block_b, _ = pairs_block.shape
    flat = pairs_block.reshape(block_d * block_b, aux)
    depth = block_d * rows_c
    steps, group = 4, block_d // 4
    occ = 8 * amp_mine.shape[1]

    def kernel(index_ref, window_ref, flat_ref, mine_ref, theirs_ref, out_ref, w, amp, ints, w_sem, amp_sem):
        g = pl.program_id(0)

        def window_copy(n):
            return pltpu.make_async_copy(window_ref.at[index_ref[n]], w.at[n], w_sem.at[n])

        def amp_copy(n):
            source = (mine_ref if n < 4 else theirs_ref).at[n % 4]
            return pltpu.make_async_copy(
                source, amp.at[pl.ds(pl.multiple_of(index_ref[12 + n] * 128, 128), 128)], amp_sem.at[n]
            )

        @pl.when(g == 0)
        def _():
            for n in range(12):
                window_copy(n).start()
            for n in range(8):
                amp_copy(n).start()
            for n in range(12):
                window_copy(n).wait()

        value = lax.dot_general(
            w[...].reshape(12 * rows_c, aux), flat_ref[...], NT, preferred_element_type=F32
        )
        low = lax.broadcasted_iota(jnp.int32, (rows_c, 128), 1) < 64
        base = pl.multiple_of(g * (group * rows_c), group * rows_c)
        for p in range(6):
            for t in range(group // 2):
                u = value[2 * p * rows_c : (2 * p + 1) * rows_c, 128 * t : 128 * (t + 1)]
                v = value[(2 * p + 1) * rows_c : (2 * p + 2) * rows_c, 128 * t : 128 * (t + 1)]
                first = jnp.where(low, u, pltpu.roll(v, 64, 1)).astype(BF)
                second = jnp.where(low, pltpu.roll(u, 64, 1), v).astype(BF)
                at = pl.ds(base + 2 * t * rows_c, rows_c)
                ints[at, 128 * p : 128 * (p + 1)] = first
                at = pl.ds(base + (2 * t + 1) * rows_c, rows_c)
                ints[at, 128 * p : 128 * (p + 1)] = second

        @pl.when(g == steps - 1)
        def _():
            for n in range(8):
                amp_copy(n).wait()

            def column(n, carry):
                at = pl.ds(pl.multiple_of(n * 256, 256), 256)
                out_ref[:, at] = jnp.dot(
                    amp[...], ints[:, at], preferred_element_type=F32
                ).astype(BF)
                return carry

            lax.fori_loop(0, 3, column, 0)

    return pl.pallas_call(
        kernel,
        grid_spec=pltpu.PrefetchScalarGridSpec(
            num_scalar_prefetch=1,
            grid=(steps,),
            in_specs=[
                pl.BlockSpec(memory_space=pl.ANY),
                pl.BlockSpec((group * block_b, aux), lambda g, i: (g, 0)),
                pl.BlockSpec(memory_space=pl.ANY),
                pl.BlockSpec(memory_space=pl.ANY),
            ],
            out_specs=pl.BlockSpec((occ, 768), lambda g, i: (0, 0)),
            scratch_shapes=[
                pltpu.VMEM((12, rows_c, aux), BF),
                pltpu.VMEM((occ, depth), BF),
                pltpu.VMEM((depth, 768), BF),
                pltpu.SemaphoreType.DMA((12,)),
                pltpu.SemaphoreType.DMA((8,)),
            ],
        ),
        out_shape=jax.ShapeDtypeStruct((occ, 768), BF),
        name="ladder_block",
    )(index, window, flat, amp_mine, amp_theirs)


def add_and_turn(parts):
    occ, lanes = parts[0].shape

    def kernel(a, b, c, d, *outs):
        total = (a[...].astype(F32) + b[...].astype(F32)) + (c[...].astype(F32) + d[...].astype(F32))
        total = total.astype(BF)
        eye = (
            lax.broadcasted_iota(jnp.int32, (128, 128), 0)
            == lax.broadcasted_iota(jnp.int32, (128, 128), 1)
        )
        eye = jnp.where(eye, 1.0, 0.0).astype(BF)
        for n in range(lanes // 128):
            turned = lax.dot_general(
                eye, total[:, n * 128 : (n + 1) * 128], NT, preferred_element_type=F32
            ).astype(BF)
            for h in range(2):
                at = n * 128 + h * 64
                outs[at // 192][at % 192 : at % 192 + 64, :] = turned[h * 64 : h * 64 + 64]

    return pl.pallas_call(
        kernel,
        grid=(occ // 256,),
        in_specs=[pl.BlockSpec((256, lanes), lambda i: (i, 0))] * 4,
        out_specs=[pl.BlockSpec((192, 256), lambda i: (0, i))] * 4,
        out_shape=[jax.ShapeDtypeStruct((192, occ), BF)] * 4,
        name="add_and_turn",
    )(*parts)


def local(
    chol_window,
    chol_pairs,
    amplitudes,
    eps_window,
    eps_virtual,
    eps_occupied,
    dress_first,
    dress_second,
):
    row, col = lax.axis_index("row"), lax.axis_index("col")
    y, core, z, x = row // 2, row % 2, col // 4, col % 4
    window_size, own_aux = chol_window.shape[0], chol_window.shape[2]
    block_b, block_d, aux = chol_pairs.shape
    occ_block = amplitudes.shape[2]
    half = window_size * window_size // 2

    own = jnp.transpose(chol_window, (2, 0, 1)).reshape(own_aux, 2 * half)
    along_y = jnp.concatenate([own] + [send(own, shift_y(s)) for s in (1, 2, 3)], axis=0)
    keep = jnp.where(core == 0, along_y[:, :half], along_y[:, half:])
    give = jnp.where(core == 0, along_y[:, half:], along_y[:, :half])
    got = send(give, swap_core)
    both = jnp.where(core == 0, jnp.stack([keep, got]), jnp.stack([got, keep]))
    both = both.reshape(8 * own_aux, half)
    plane = jnp.stack([both] + [send(both, shift_first(s)) for s in (1, 2, 3)])
    mine = [plane] + [send(plane, shift_second(s)) for s in (1, 2, 3)]
    theirs = [send(piece, swap_core) for piece in mine]
    window = turn_window(mine, theirs).reshape(window_size, window_size, aux)

    amp = jnp.transpose(amplitudes, (2, 1, 0)).reshape(occ_block, block_d * window_size)
    amp_mine = jnp.stack([amp] + [send(amp, shift_y(s)) for s in (1, 2, 3)])
    amp_theirs = send(amp_mine, swap_core)

    k = jnp.arange(aux, dtype=jnp.int32)
    i, slot = k % own_aux, k // own_aux
    s_y, c, v, u = slot % 4, (slot // 4) % 2, (slot // 8) % 4, slot // 32
    k_z = jnp.where(core == 0, z - v, z - u) % 4
    k_x = jnp.where(core == 0, x - u, x - v) % 4
    order = (((((y - s_y) % 4) * 2 + c) * 4 + k_z) * 4 + k_x) * own_aux + i
    pairs_block = prepare_pairs(chol_pairs, order.astype(jnp.int32)[None, :])

    n = jnp.arange(12, dtype=jnp.int32)
    s = jnp.arange(4, dtype=jnp.int32)
    amp_at = jnp.concatenate([((y - s) % 4) * 2 + core, ((y - s) % 4) * 2 + 1 - core])

    def block(shift):
        a = jnp.where(
            core == 0,
            12 * ((z + shift) % 4) + 3 * ((x + n // 3) % 4) + n % 3,
            12 * ((z + n // 3) % 4) + 3 * ((x + shift) % 4) + n % 3,
        )
        a = (jnp.where(a >= window_size // 2, 1 - core, core)) * (window_size // 2) + a % (
            window_size // 2
        )
        index = jnp.concatenate([a, amp_at]).astype(jnp.int32)
        return ladder_block(index, window, pairs_block, amp_mine, amp_theirs)

    parts = []
    for shift in (2, 1, 3):
        parts.append(send(block(shift), shift_first(shift)))
    parts.append(block(0))
    pieces = add_and_turn(parts)
    summed = pieces[0].astype(F32)
    for shift in (1, 2, 3):
        summed = summed + send(pieces[shift], shift_second(shift)).astype(F32)

    occ_count = summed.shape[1]
    rows_a = eps_window.shape[0]
    denominator = (
        eps_window[:, None, None] + eps_virtual[None, :, None] + eps_occupied[None, None, :]
    ).reshape(rows_a * block_b, occ_count)
    flattened = (summed / denominator).astype(BF)
    first_mix = jnp.dot(flattened, dress_first, preferred_element_type=F32).astype(BF)
    mixed = flattened.astype(F32) + jnp.dot(first_mix, dress_second, preferred_element_type=F32)
    mixed = mixed.astype(BF).reshape(rows_a, block_b, occ_count)
    return lax.all_to_all(mixed, "row", split_axis=2, concat_axis=1, tiled=True)


def solution(mesh):
    return jax.shard_map(
        local,
        mesh=mesh,
        in_specs=(
            P(None, None, ("row", "col")),
            P("row", "col", None),
            P(None, "col", "row"),
            P("col"),
            P("row"),
            P(),
            P(),
            P(),
        ),
        out_specs=P("col", None, "row"),
        check_vma=False,
    )
```

```python
import functools

import jax
import jax.numpy as jnp
from jax import lax
from jax.experimental import pallas as pl
from jax.experimental.pallas import tpu as pltpu
from jax.sharding import PartitionSpec as P

AXES = ("row", "col")
BF = jnp.bfloat16
F32 = jnp.float32
NT = (((1,), (1,)), ((), ()))


def linear(y, c, z, x):
    return (((y % 4) * 2 + c % 2) * 4 + z % 4) * 4 + x % 4


def pairs(move):
    return [
        (linear(y, c, z, x), linear(*move(y, c, z, x)))
        for y in range(4)
        for c in range(2)
        for z in range(4)
        for x in range(4)
    ]


def send(value, move):
    return lax.ppermute(value, AXES, pairs(move))


def shift_y(s):
    return lambda y, c, z, x: (y + s, c, z, x)


def swap_core(y, c, z, x):
    return (y, 1 - c, z, x)


def shift_first(s):
    return lambda y, c, z, x: (y, c, z + s * (1 - c), x + s * c)


def shift_second(s):
    return lambda y, c, z, x: (y, c, z + s * c, x + s * (1 - c))


def move_row(s, c):
    return lambda y, core, z, x: (y + s, core + c, z, x)


def after(value, *others):
    return lax.optimization_barrier((value, *others))[0]


VMEM_SPEC = pl.BlockSpec(memory_space=pltpu.VMEM)
SMEM_SPEC = pl.BlockSpec(memory_space=pltpu.SMEM)
LIMIT = pltpu.CompilerParams(vmem_limit_bytes=20 * 1024 * 1024)


def in_vmem(value):
    return pltpu.with_memory_space_constraint(value, pltpu.VMEM)


def out_vmem(*shape):
    return pltpu.VMEM(shape, BF)


def cost(flops, moved):
    return pl.CostEstimate(flops=flops, transcendentals=0, bytes_accessed=moved)


def one_hot_eye():
    eye = (
        lax.broadcasted_iota(jnp.int32, (128, 128), 0)
        == lax.broadcasted_iota(jnp.int32, (128, 128), 1)
    )
    return jnp.where(eye, 1.0, 0.0).astype(BF)


def prepare_pairs(chol_pairs, order, part):
    block_b, block_d, aux = chol_pairs.shape

    def kernel(order_ref, in_ref, out_ref, columns):
        @pl.when(pl.program_id(0) == 0)
        def _():
            q = lax.broadcasted_iota(jnp.int32, (aux, aux), 0)
            columns[...] = jnp.where(q == order_ref[...], 1.0, 0.0).astype(BF)

        target = lax.broadcasted_iota(jnp.int32, (256, 256), 0)
        source = lax.broadcasted_iota(jnp.int32, (256, 256), 1)
        rows = jnp.where((target % 16) * 16 + target // 16 == source, 1.0, 0.0).astype(BF)
        block = in_ref[...].reshape(256, aux)
        block = jnp.dot(rows, block, preferred_element_type=F32).astype(BF)
        block = jnp.dot(block, columns[...], preferred_element_type=F32).astype(BF)
        at = pl.ds(pl.multiple_of(pl.program_id(0) * 16, 16), 16)
        out_ref[:, at, :] = block.reshape(16, 16, aux)

    return pl.pallas_call(
        kernel,
        grid=(block_b // 16,),
        in_specs=[VMEM_SPEC, pl.BlockSpec((16, 16, aux), lambda i: (i, part, 0))],
        out_specs=VMEM_SPEC,
        out_shape=out_vmem(16, block_b, aux),
        scratch_shapes=[pltpu.VMEM((aux, aux), BF)],
        cost_estimate=cost(block_b * block_d * aux * (aux + 256), 2 * block_b * block_d * aux),
        compiler_params=LIMIT,
        name="prepare_pairs",
    )(order, chol_pairs)


def turn_window(mine, theirs):
    lanes = mine[0].shape[2]
    aux = 4 * 4 * 96

    def kernel(*refs):
        mine_refs, their_refs, out_ref = refs[:4], refs[4:8], refs[8]
        eye = one_hot_eye()

        def put(value, base, slot):
            turned = lax.dot_general(eye, value, NT, preferred_element_type=F32)
            rows = pl.ds(pl.multiple_of(base, 128), 128)
            out_ref[rows, slot * 384 : (slot + 1) * 384] = turned.astype(BF)

        def columns(n, carry):
            at = pl.ds(pl.multiple_of(n * 128, 128), 128)
            for s in range(4):
                put(mine_refs[s][:, :, at].reshape(384, 128), n * 128, s)
            for m in range(4):
                value = jnp.concatenate([their_refs[s][m, :, at] for s in range(4)], axis=0)
                put(value, lanes + n * 128, m)
            return carry

        lax.fori_loop(0, lanes // 128, columns, 0)

    return pl.pallas_call(
        kernel,
        in_specs=[VMEM_SPEC] * 8,
        out_specs=VMEM_SPEC,
        out_shape=out_vmem(2 * lanes, aux),
        cost_estimate=cost(2 * 2 * lanes * aux * 256, 8 * lanes * aux),
        compiler_params=LIMIT,
        name="turn_window",
    )(*[in_vmem(p) for p in mine], *[in_vmem(p) for p in theirs])


def ladder_block(index, window, pairs_parts, amp_mine, amp_theirs, first):
    rows_c, aux = window.shape[1], window.shape[2]
    part_d, block_b, _ = pairs_parts[0].shape
    flats = [p.reshape(part_d * block_b, aux) for p in pairs_parts]
    depth = 2 * part_d * rows_c
    group = part_d // 2
    count = 16
    rows_o = amp_mine.shape[1]
    occ = 8 * rows_o

    def kernel(index_ref, window_ref, flat0, flat1, mine_ref, theirs_ref, o0, o1, o2, o3, w, ints, out):
        outs = (o0, o1, o2, o3)
        for n in range(count):
            w[n * rows_c : (n + 1) * rows_c, :] = window_ref[index_ref[first + n]]
        low = lax.broadcasted_iota(jnp.int32, (rows_c, 128), 1) < 64

        for g in range(4):
            at = slice((g % 2) * group * block_b, (g % 2 + 1) * group * block_b)
            right = (flat0, flat1)[g // 2][at, :]
            value = lax.dot_general(w[...], right, NT, preferred_element_type=F32)
            for p in range(count // 2):
                for t in range(group // 2):
                    u = value[2 * p * rows_c : (2 * p + 1) * rows_c, 128 * t : 128 * (t + 1)]
                    v = value[(2 * p + 1) * rows_c : (2 * p + 2) * rows_c, 128 * t : 128 * (t + 1)]
                    one = jnp.where(low, u, pltpu.roll(v, 64, 1)).astype(BF)
                    two = jnp.where(low, pltpu.roll(u, 64, 1), v).astype(BF)
                    base = (g * group + 2 * t) * rows_c
                    ints[base : base + rows_c, 128 * p : 128 * (p + 1)] = one
                    ints[base + rows_c : base + 2 * rows_c, 128 * p : 128 * (p + 1)] = two

        def product(n, carry):
            right = ints[:, pl.ds(pl.multiple_of(n * 256, 256), 256)]
            for k, ref in enumerate((mine_ref, theirs_ref)):
                left = ref[...].reshape(4 * rows_o, depth)
                value = jnp.dot(left, right, preferred_element_type=F32).astype(BF)
                for m in range(4):
                    rows = pl.ds(pl.multiple_of(index_ref[4 * k + m] * rows_o, rows_o), rows_o)
                    out[rows, :] = value[m * rows_o : (m + 1) * rows_o]
            for j in range(4):

                @pl.when(n == j)
                def _():
                    outs[j][...] = out[...]

            return carry

        lax.fori_loop(0, 4, product, 0)

    return pl.pallas_call(
        kernel,
        in_specs=[SMEM_SPEC] + [VMEM_SPEC] * 5,
        out_specs=[VMEM_SPEC] * 4,
        scratch_shapes=[
            pltpu.VMEM((count * rows_c, aux), BF),
            pltpu.VMEM((depth, count * block_b), BF),
            pltpu.VMEM((occ, 4 * block_b), BF),
        ],
        out_shape=[out_vmem(occ, 4 * block_b)] * 4,
        cost_estimate=cost(2 * count * rows_c * depth * block_b * (aux + occ) // rows_c, 2000000),
        compiler_params=LIMIT,
        name="ladder_block",
    )(index, in_vmem(window), *[in_vmem(f) for f in flats], in_vmem(amp_mine), in_vmem(amp_theirs))


def add_and_turn(groups):
    occ, lanes = groups[0][0].shape
    many = len(groups)

    def kernel(*refs):
        outs = refs[4 * many :]
        eye = one_hot_eye()
        for j in range(many):
            p = refs[4 * j : 4 * j + 4]
            total = (p[0][...].astype(F32) + p[1][...].astype(F32)) + (
                p[2][...].astype(F32) + p[3][...].astype(F32)
            )
            total = total.astype(BF)
            for n in range(lanes // 128):
                turned = lax.dot_general(
                    eye, total[:, n * 128 : (n + 1) * 128], NT, preferred_element_type=F32
                ).astype(BF)
                for h in range(2):
                    outs[2 * n + h][64 * j : 64 * j + 64, :] = turned[h * 64 : h * 64 + 64]

    return pl.pallas_call(
        kernel,
        in_specs=[VMEM_SPEC] * (4 * many),
        out_specs=[VMEM_SPEC] * 4,
        out_shape=[out_vmem(64 * many, occ)] * 4,
        cost_estimate=cost(2 * occ * lanes * 256, 3000000),
        compiler_params=LIMIT,
        name="add_and_turn",
    )(*[in_vmem(p) for group in groups for p in group])


def dress(index, pieces, eps_pair, eps_occupied, dress_first, dress_second):
    rows, occ = eps_pair.shape[0], eps_occupied.shape[1]
    rows_b = 64
    rows_a = rows // rows_b
    heights = [group[0].shape[0] for group in pieces]

    def kernel(index_ref, *refs):
        ins, refs = refs[: 4 * len(pieces)], refs[4 * len(pieces) :]
        pair_ref, occ_ref, first_ref, second_ref = refs[:4]
        outs, (ladder, mixed, right, sem) = refs[4:12], refs[12:]
        copies = [
            pltpu.make_async_copy(ref, right.at[n], sem.at[n])
            for n, ref in enumerate((first_ref, second_ref))
        ]
        for copy in copies:
            copy.start()
        base = 0
        for n, height in enumerate(heights):
            p = [ref[...].astype(F32) for ref in ins[4 * n : 4 * n + 4]]
            ladder[base : base + height, :] = (p[0] + p[1]) + (p[2] + p[3])
            base += height
        scaled = (ladder[...] / (pair_ref[...] + occ_ref[...])).astype(BF)
        copies[0].wait()
        first = jnp.dot(scaled, right[0], preferred_element_type=F32).astype(BF)
        copies[1].wait()
        second = jnp.dot(first, right[1], preferred_element_type=F32)
        mixed[...] = scaled.astype(F32) + second
        for n in range(8):
            at = pl.ds(pl.multiple_of(index_ref[8 + n] * 128, 128), 128)
            outs[n][...] = mixed[:, at].astype(BF).reshape(rows_a, rows_b, 128)

    flat = [in_vmem(p) for group in pieces for p in group]
    return pl.pallas_call(
        kernel,
        in_specs=[SMEM_SPEC] + [VMEM_SPEC] * (len(flat) + 2) + [pl.BlockSpec(memory_space=pltpu.HBM)] * 2,
        out_specs=[VMEM_SPEC] * 8,
        out_shape=[out_vmem(rows_a, rows_b, 128)] * 8,
        scratch_shapes=[
            pltpu.VMEM((rows, occ), F32),
            pltpu.VMEM((rows, occ), F32),
            pltpu.VMEM((2, occ, occ), BF),
            pltpu.SemaphoreType.DMA((2,)),
        ],
        cost_estimate=cost(4 * rows * occ * occ, 6000000),
        compiler_params=LIMIT,
        name="dress",
    )(index, *flat, eps_pair, eps_occupied, dress_first, dress_second)


def place(index, blocks):
    rows_a, rows_b, lanes = blocks[0].shape

    def kernel(index_ref, *refs):
        for n in range(8):
            at = pl.ds(pl.multiple_of(index_ref[n] * rows_b, rows_b), rows_b)
            refs[8][:, at, :] = refs[n][...]

    return pl.pallas_call(
        kernel,
        in_specs=[SMEM_SPEC] + [VMEM_SPEC] * 8,
        out_specs=VMEM_SPEC,
        out_shape=jax.ShapeDtypeStruct((rows_a, 8 * rows_b, lanes), BF),
        compiler_params=LIMIT,
        name="place",
    )(index, *[in_vmem(p) for p in blocks])


def local(
    chol_window,
    chol_pairs,
    amplitudes,
    eps_window,
    eps_virtual,
    eps_occupied,
    dress_first,
    dress_second,
):
    row, col = lax.axis_index("row"), lax.axis_index("col")
    y, core, z, x = row // 2, row % 2, col // 4, col % 4
    window_size, own_aux = chol_window.shape[0], chol_window.shape[2]
    block_b, block_d, aux = chol_pairs.shape
    occ_block = amplitudes.shape[2]
    rows_a = window_size // 16
    part = 8 * window_size
    shifts = (1, 2, 3)

    own = jnp.transpose(chol_window.reshape(2, 8, rows_a, window_size, own_aux), (4, 0, 2, 1, 3))
    own = own.reshape(own_aux, 2 * rows_a * part)
    sent = [send(own, shift_y(s)) for s in shifts]

    k = jnp.arange(aux, dtype=jnp.int32)
    i, slot = k % own_aux, k // own_aux
    s_y, c, v, u = slot % 4, (slot // 4) % 2, (slot // 8) % 4, slot // 32
    k_z = jnp.where(core == 0, z - v, z - u) % 4
    k_x = jnp.where(core == 0, x - u, x - v) % 4
    order = (((((y - s_y) % 4) * 2 + c) * 4 + k_z) * 4 + k_x) * own_aux + i
    order = order.astype(jnp.int32)[None, :]
    amp = jnp.transpose(amplitudes, (2, 1, 0)).reshape(occ_block, block_d * window_size)

    n = jnp.arange(16, dtype=jnp.int32)
    s = jnp.arange(4, dtype=jnp.int32)
    owner = jnp.where(
        core == 0,
        4 * ((z + n // 4) % 4) + (x + n % 4) % 4,
        4 * ((z + n % 4) % 4) + (x + n // 4) % 4,
    )
    other = jnp.where(owner // 8 == core, 0, 1)
    index = [((y - s) % 4) * 2 + core, ((y - s) % 4) * 2 + 1 - core]
    index += [((y + s) % 4) * 2 + core, ((y + s) % 4) * 2 + 1 - core]
    for group, at in ((1, 0), (rows_a - 1, 0), (rows_a - 1, 1)):
        index.append((other * group + at) * 8 + owner % 8)
    index = jnp.concatenate(index).astype(jnp.int32)
    eps_pair = (eps_window[:, None] + eps_virtual[None, :]).reshape(rows_a * block_b, 1)
    amp_sent = [send(amp, shift_y(s)) for s in shifts]
    sent[0], index, eps_pair, order = lax.optimization_barrier((sent[0], index, eps_pair, order))

    along_y = jnp.concatenate([own] + sent, axis=0)
    half = rows_a * part
    keep = jnp.where(core == 0, along_y[:, :half], along_y[:, half:])
    give = jnp.where(core == 0, along_y[:, half:], along_y[:, :half])
    got = send(give, swap_core)
    both = jnp.where(core == 0, jnp.stack([keep, got]), jnp.stack([got, keep]))
    both = both.reshape(8 * own_aux, half)
    plane = [send(both, shift_first(s)) for s in shifts]

    pairs_one = prepare_pairs(chol_pairs, after(order, both), 0)
    *plane, pairs_one = lax.optimization_barrier((*plane, pairs_one))
    plane = [both] + plane

    groups = []
    for start, stop in ((0, 1), (1, rows_a)):
        piece = jnp.stack([p[:, start * part : stop * part] for p in plane])
        groups.append([piece] + [send(piece, shift_second(s)) for s in shifts])
    swapped = [send(group[0], swap_core) for group in groups]
    amp_mine = jnp.stack([amp] + amp_sent)
    amp_theirs = send(amp_mine, swap_core)
    pairs_two = prepare_pairs(
        chol_pairs, after(order, groups[1][0], pairs_one, amp_mine), 1
    )
    *groups[0], pairs_two = lax.optimization_barrier((*groups[0], pairs_two))

    def turn(group, first):
        theirs = [first] + [send(p, swap_core) for p in group[1:]]
        turned = turn_window(group, theirs)
        return turned.reshape(turned.shape[0] // window_size, window_size, aux)

    window = turn(groups[0], swapped[0])

    pieces, parts = [], []
    for a in range(rows_a):
        if a == 1:
            groups[1] = lax.optimization_barrier((*groups[1], *parts[0]))[:4]
            window = turn(groups[1], swapped[1])
        if a == 2:
            window = after(window, *parts[1])
        outs = ladder_block(
            index, window, (pairs_one, pairs_two), amp_mine, amp_theirs, 16 + 16 * a
        )
        parts.append(outs)
    for group in ([0, 1], [2]):
        sums = []
        for a in group:
            sums.append([parts[a][0]] + [send(parts[a][m], shift_first(m)) for m in shifts])
        mine = add_and_turn(sums)
        pieces.append([mine[0]] + [send(mine[m], shift_second(m)) for m in shifts])

    blocks = dress(index, pieces, eps_pair, eps_occupied[None, :], dress_first, dress_second)
    blocks = [blocks[0]] + [send(blocks[m], move_row(m % 4, m // 4)) for m in range(1, 8)]
    return place(index, blocks)


def solution(mesh):
    return jax.shard_map(
        local,
        mesh=mesh,
        in_specs=(
            P(None, None, ("row", "col")),
            P("row", "col", None),
            P(None, "col", "row"),
            P("col"),
            P("row"),
            P(),
            P(),
            P(),
        ),
        out_specs=P("col", None, "row"),
        check_vma=False,
    )
```

```python
import functools

import jax
import jax.numpy as jnp
from jax import lax
from jax.experimental import pallas as pl
from jax.experimental.pallas import tpu as pltpu
from jax.sharding import PartitionSpec as P

AXES = ("row", "col")
BF = jnp.bfloat16
F32 = jnp.float32
NT = (((1,), (1,)), ((), ()))


def linear(y, c, z, x):
    return (((y % 4) * 2 + c % 2) * 4 + z % 4) * 4 + x % 4


def pairs(move):
    return [
        (linear(y, c, z, x), linear(*move(y, c, z, x)))
        for y in range(4)
        for c in range(2)
        for z in range(4)
        for x in range(4)
    ]


def send(value, move):
    return lax.ppermute(value, AXES, pairs(move))


def shift_y(s):
    return lambda y, c, z, x: (y + s, c, z, x)


def swap_core(y, c, z, x):
    return (y, 1 - c, z, x)


def shift_first(s):
    return lambda y, c, z, x: (y, c, z + s * (1 - c), x + s * c)


def shift_second(s):
    return lambda y, c, z, x: (y, c, z + s * c, x + s * (1 - c))


def move_row(s, c):
    return lambda y, core, z, x: (y + s, core + c, z, x)


def after(value, *others):
    return lax.optimization_barrier((value, *others))[0]


VMEM_SPEC = pl.BlockSpec(memory_space=pltpu.VMEM)
SMEM_SPEC = pl.BlockSpec(memory_space=pltpu.SMEM)
LIMIT = pltpu.CompilerParams(vmem_limit_bytes=20 * 1024 * 1024)


def in_vmem(value):
    return pltpu.with_memory_space_constraint(value, pltpu.VMEM)


def in_hbm(value):
    return pltpu.with_memory_space_constraint(value, pltpu.HBM)


def out_vmem(*shape):
    return pltpu.VMEM(shape, BF)


def cost(flops, moved):
    return pl.CostEstimate(flops=flops, transcendentals=0, bytes_accessed=moved)


def one_hot_eye():
    eye = (
        lax.broadcasted_iota(jnp.int32, (128, 128), 0)
        == lax.broadcasted_iota(jnp.int32, (128, 128), 1)
    )
    return jnp.where(eye, 1.0, 0.0).astype(BF)


def prepare_pairs(chol_pairs, order, part):
    block_b, block_d, aux = chol_pairs.shape

    def kernel(order_ref, in_ref, out_ref, columns):
        @pl.when(pl.program_id(0) == 0)
        def _():
            q = lax.broadcasted_iota(jnp.int32, (aux, aux), 0)
            columns[...] = jnp.where(q == order_ref[...], 1.0, 0.0).astype(BF)

        target = lax.broadcasted_iota(jnp.int32, (256, 256), 0)
        source = lax.broadcasted_iota(jnp.int32, (256, 256), 1)
        rows = jnp.where((target % 16) * 16 + target // 16 == source, 1.0, 0.0).astype(BF)
        block = in_ref[...].reshape(256, aux)
        block = jnp.dot(rows, block, preferred_element_type=F32).astype(BF)
        block = jnp.dot(block, columns[...], preferred_element_type=F32).astype(BF)
        at = pl.ds(pl.multiple_of(pl.program_id(0) * 16, 16), 16)
        out_ref[:, at, :] = block.reshape(16, 16, aux)

    return pl.pallas_call(
        kernel,
        grid=(block_b // 16,),
        in_specs=[VMEM_SPEC, pl.BlockSpec((16, 16, aux), lambda i: (i, part, 0))],
        out_specs=VMEM_SPEC,
        out_shape=out_vmem(16, block_b, aux),
        scratch_shapes=[pltpu.VMEM((aux, aux), BF)],
        cost_estimate=cost(block_b * block_d * aux * (aux + 256), 2 * block_b * block_d * aux),
        compiler_params=LIMIT,
        name="prepare_pairs",
    )(order, chol_pairs)


def turn_window(mine, theirs):
    depth, lanes = mine[0].shape[1:]
    aux = 32 * depth
    pieces = [*mine, *theirs]

    def kernel(*refs):
        out_ref = refs[8]
        eye = one_hot_eye()

        def columns(n, carry):
            at = pl.ds(pl.multiple_of(n * 128, 128), 128)
            for j in range(4):
                value = [refs[2 * j + m][:, :, at].reshape(4 * depth, 128) for m in range(2)]
                value = jnp.concatenate(value, axis=0)
                turned = lax.dot_general(eye, value, NT, preferred_element_type=F32)
                out_ref[at, 8 * depth * j : 8 * depth * (j + 1)] = turned.astype(BF)
            return carry

        lax.fori_loop(0, lanes // 128, columns, 0)

    return pl.pallas_call(
        kernel,
        in_specs=[VMEM_SPEC] * 8,
        out_specs=VMEM_SPEC,
        out_shape=out_vmem(lanes, aux),
        cost_estimate=cost(2 * lanes * aux * 256, 4 * lanes * aux),
        compiler_params=LIMIT,
        name="turn_window",
    )(*[in_vmem(p) for p in pieces])


def ladder_block(index, window, pairs_parts, amp_mine, amp_theirs, first):
    rows_c, aux = window.shape[1], window.shape[2]
    part_d, block_b, _ = pairs_parts[0].shape
    flats = [p.reshape(part_d * block_b, aux) for p in pairs_parts]
    depth = 2 * part_d * rows_c
    group = part_d // 2
    count = 16
    rows_o = amp_mine.shape[1]
    occ = 8 * rows_o

    def kernel(index_ref, window_ref, flat0, flat1, mine_ref, theirs_ref, o0, o1, o2, o3, w, ints, out):
        outs = (o0, o1, o2, o3)
        for n in range(count):
            w[n * rows_c : (n + 1) * rows_c, :] = window_ref[index_ref[first + n]]
        low = lax.broadcasted_iota(jnp.int32, (rows_c, 128), 1) < 64

        for g in range(4):
            at = slice((g % 2) * group * block_b, (g % 2 + 1) * group * block_b)
            right = (flat0, flat1)[g // 2][at, :]
            value = lax.dot_general(w[...], right, NT, preferred_element_type=F32)
            for p in range(count // 2):
                for t in range(group // 2):
                    u = value[2 * p * rows_c : (2 * p + 1) * rows_c, 128 * t : 128 * (t + 1)]
                    v = value[(2 * p + 1) * rows_c : (2 * p + 2) * rows_c, 128 * t : 128 * (t + 1)]
                    one = jnp.where(low, u, pltpu.roll(v, 64, 1)).astype(BF)
                    two = jnp.where(low, pltpu.roll(u, 64, 1), v).astype(BF)
                    base = (g * group + 2 * t) * rows_c
                    ints[base : base + rows_c, 128 * p : 128 * (p + 1)] = one
                    ints[base + rows_c : base + 2 * rows_c, 128 * p : 128 * (p + 1)] = two

        def product(n, carry):
            right = ints[:, pl.ds(pl.multiple_of(n * 256, 256), 256)]
            for k, ref in enumerate((mine_ref, theirs_ref)):
                left = ref[...].reshape(4 * rows_o, depth)
                value = jnp.dot(left, right, preferred_element_type=F32).astype(BF)
                for m in range(4):
                    rows = pl.ds(pl.multiple_of(index_ref[4 * k + m] * rows_o, rows_o), rows_o)
                    out[rows, :] = value[m * rows_o : (m + 1) * rows_o]
            for j in range(4):

                @pl.when(n == j)
                def _():
                    outs[j][...] = out[...]

            return carry

        lax.fori_loop(0, 4, product, 0)

    return pl.pallas_call(
        kernel,
        in_specs=[SMEM_SPEC] + [VMEM_SPEC] * 5,
        out_specs=[VMEM_SPEC] * 4,
        scratch_shapes=[
            pltpu.VMEM((count * rows_c, aux), BF),
            pltpu.VMEM((depth, count * block_b), BF),
            pltpu.VMEM((occ, 4 * block_b), BF),
        ],
        out_shape=[out_vmem(occ, 4 * block_b)] * 4,
        cost_estimate=cost(2 * count * rows_c * depth * block_b * (aux + occ) // rows_c, 2000000),
        compiler_params=LIMIT,
        name="ladder_block",
    )(index, in_vmem(window), *[in_vmem(f) for f in flats], in_vmem(amp_mine), in_vmem(amp_theirs))


def add_and_turn(groups):
    occ, lanes = groups[0][0].shape
    many = len(groups)

    def kernel(*refs):
        outs = refs[4 * many :]
        eye = one_hot_eye()
        for j in range(many):
            p = refs[4 * j : 4 * j + 4]
            total = (p[0][...].astype(F32) + p[1][...].astype(F32)) + (
                p[2][...].astype(F32) + p[3][...].astype(F32)
            )
            total = total.astype(BF)
            for n in range(lanes // 128):
                turned = lax.dot_general(
                    eye, total[:, n * 128 : (n + 1) * 128], NT, preferred_element_type=F32
                ).astype(BF)
                for h in range(2):
                    outs[2 * n + h][64 * j : 64 * j + 64, :] = turned[h * 64 : h * 64 + 64]

    return pl.pallas_call(
        kernel,
        in_specs=[VMEM_SPEC] * (4 * many),
        out_specs=[VMEM_SPEC] * 4,
        out_shape=[out_vmem(64 * many, occ)] * 4,
        cost_estimate=cost(2 * occ * lanes * 256, 3000000),
        compiler_params=LIMIT,
        name="add_and_turn",
    )(*[in_vmem(p) for group in groups for p in group])


def dress(index, pieces, eps_pair, eps_occupied, dress_first, dress_second):
    rows, occ = eps_pair.shape[0], eps_occupied.shape[1]
    rows_b = 64
    rows_a = rows // rows_b
    heights = [group[0].shape[0] for group in pieces]

    def kernel(index_ref, *refs):
        ins, refs = refs[: 4 * len(pieces)], refs[4 * len(pieces) :]
        pair_ref, occ_ref, first_ref, second_ref = refs[:4]
        outs, (ladder, mixed, right, sem) = refs[4:12], refs[12:]
        copies = [
            pltpu.make_async_copy(ref, right.at[n], sem.at[n])
            for n, ref in enumerate((first_ref, second_ref))
        ]
        for copy in copies:
            copy.start()
        base = 0
        for n, height in enumerate(heights):
            p = [ref[...].astype(F32) for ref in ins[4 * n : 4 * n + 4]]
            ladder[base : base + height, :] = (p[0] + p[1]) + (p[2] + p[3])
            base += height
        scaled = (ladder[...] / (pair_ref[...] + occ_ref[...])).astype(BF)
        copies[0].wait()
        first = jnp.dot(scaled, right[0], preferred_element_type=F32).astype(BF)
        copies[1].wait()
        second = jnp.dot(first, right[1], preferred_element_type=F32)
        mixed[...] = scaled.astype(F32) + second
        for n in range(8):
            at = pl.ds(pl.multiple_of(index_ref[8 + n] * 128, 128), 128)
            outs[n][...] = mixed[:, at].astype(BF).reshape(rows_a, rows_b, 128)

    flat = [in_vmem(p) for group in pieces for p in group]
    return pl.pallas_call(
        kernel,
        in_specs=[SMEM_SPEC] + [VMEM_SPEC] * (len(flat) + 2) + [pl.BlockSpec(memory_space=pltpu.HBM)] * 2,
        out_specs=[VMEM_SPEC] * 8,
        out_shape=[out_vmem(rows_a, rows_b, 128)] * 8,
        scratch_shapes=[
            pltpu.VMEM((rows, occ), F32),
            pltpu.VMEM((rows, occ), F32),
            pltpu.VMEM((2, occ, occ), BF),
            pltpu.SemaphoreType.DMA((2,)),
        ],
        cost_estimate=cost(4 * rows * occ * occ, 6000000),
        compiler_params=LIMIT,
        name="dress",
    )(index, *flat, eps_pair, eps_occupied, in_hbm(dress_first), in_hbm(dress_second))


def place(index, blocks):
    rows_a, rows_b, lanes = blocks[0].shape

    def kernel(index_ref, *refs):
        for n in range(8):
            at = pl.ds(pl.multiple_of(index_ref[n] * rows_b, rows_b), rows_b)
            refs[8][:, at, :] = refs[n][...]

    return pl.pallas_call(
        kernel,
        in_specs=[SMEM_SPEC] + [VMEM_SPEC] * 8,
        out_specs=VMEM_SPEC,
        out_shape=jax.ShapeDtypeStruct((rows_a, 8 * rows_b, lanes), BF),
        compiler_params=LIMIT,
        name="place",
    )(index, *[in_vmem(p) for p in blocks])


def local(
    chol_window,
    chol_pairs,
    amplitudes,
    eps_window,
    eps_virtual,
    eps_occupied,
    dress_first,
    dress_second,
):
    row, col = lax.axis_index("row"), lax.axis_index("col")
    y, core, z, x = row // 2, row % 2, col // 4, col % 4
    window_size, own_aux = chol_window.shape[0], chol_window.shape[2]
    block_b, block_d, aux = chol_pairs.shape
    occ_block = amplitudes.shape[2]
    rows_a = window_size // 16
    part = 16 * window_size
    shifts = (1, 2, 3)

    own = jnp.transpose(chol_window.reshape(16, rows_a, window_size, own_aux), (3, 1, 0, 2))
    own = own.reshape(own_aux, rows_a * part)
    sent = [send(own, shift_y(s)) for s in shifts]

    k = jnp.arange(aux, dtype=jnp.int32)
    i, slot = k % own_aux, k // own_aux
    s_y, v, u, c = slot % 4, (slot // 4) % 4, (slot // 16) % 4, (core + slot // 64) % 2
    k_z = jnp.where(c == 0, z - v, z - u) % 4
    k_x = jnp.where(c == 0, x - u, x - v) % 4
    order = (((((y - s_y) % 4) * 2 + c) * 4 + k_z) * 4 + k_x) * own_aux + i
    order = order.astype(jnp.int32)[None, :]
    amp = jnp.transpose(amplitudes, (2, 1, 0)).reshape(occ_block, block_d * window_size)

    n = jnp.arange(16, dtype=jnp.int32)
    s = jnp.arange(4, dtype=jnp.int32)
    owner = jnp.where(
        core == 0,
        4 * ((z + n // 4) % 4) + (x + n % 4) % 4,
        4 * ((z + n % 4) % 4) + (x + n // 4) % 4,
    )
    index = [((y - s) % 4) * 2 + core, ((y - s) % 4) * 2 + 1 - core]
    index += [((y + s) % 4) * 2 + core, ((y + s) % 4) * 2 + 1 - core]
    index += [owner, owner, owner + 16]
    index = jnp.concatenate(index).astype(jnp.int32)
    eps_pair = (eps_window[:, None] + eps_virtual[None, :]).reshape(rows_a * block_b, 1)
    amp_sent = [send(amp, shift_y(s)) for s in shifts]
    sent[0], index, eps_pair, order, amp = lax.optimization_barrier(
        (sent[0], index, eps_pair, order, amp)
    )

    both = jnp.concatenate([own] + sent, axis=0)
    plane = [send(both, shift_first(s)) for s in shifts]

    chol_pairs = in_hbm(chol_pairs)
    pairs_one = prepare_pairs(chol_pairs, after(order, both), 0)
    *plane, pairs_one = lax.optimization_barrier((*plane, pairs_one))
    plane = [both] + plane

    groups = []
    for start, stop in ((0, 1), (1, rows_a)):
        piece = jnp.stack([p[:, start * part : stop * part] for p in plane])
        groups.append([piece] + [send(piece, shift_second(s)) for s in shifts])
    swapped = [send(group[0], swap_core) for group in groups]
    amp_mine = jnp.stack([amp] + amp_sent)
    amp_theirs = send(amp_mine, swap_core)
    pairs_two = prepare_pairs(
        chol_pairs, after(order, groups[1][0], pairs_one, amp_mine), 1
    )
    *groups[0], pairs_two = lax.optimization_barrier((*groups[0], pairs_two))

    def turn(group, first):
        theirs = [first] + [send(p, swap_core) for p in group[1:]]
        turned = turn_window(group, theirs)
        return turned.reshape(turned.shape[0] // window_size, window_size, aux)

    window = turn(groups[0], swapped[0])

    pieces, parts = [], []
    for a in range(rows_a):
        if a == 1:
            groups[1] = lax.optimization_barrier((*groups[1], *parts[0]))[:4]
            window = turn(groups[1], swapped[1])
        if a == 2:
            window = after(window, *parts[1])
        outs = ladder_block(
            index, window, (pairs_one, pairs_two), amp_mine, amp_theirs, 16 + 16 * a
        )
        parts.append(outs)
    for group in ([0, 1], [2]):
        sums = []
        for a in group:
            sums.append([parts[a][0]] + [send(parts[a][m], shift_first(m)) for m in (2, 1, 3)])
        mine = add_and_turn(sums)
        pieces.append([mine[0]] + [send(mine[m], shift_second(m)) for m in (2, 1, 3)])

    blocks = dress(index, pieces, eps_pair, eps_occupied[None, :], dress_first, dress_second)
    blocks = [blocks[0]] + [send(blocks[m], move_row(m % 4, m // 4)) for m in range(1, 8)]
    return place(index, blocks)


def solution(mesh):
    return jax.shard_map(
        local,
        mesh=mesh,
        in_specs=(
            P(None, None, ("row", "col")),
            P("row", "col", None),
            P(None, "col", "row"),
            P("col"),
            P("row"),
            P(),
            P(),
            P(),
        ),
        out_specs=P("col", None, "row"),
        check_vma=False,
    )
```

```python
import jax
import jax.numpy as jnp
from jax import lax
from jax.experimental import pallas as pl
from jax.experimental.pallas import tpu as pltpu
from jax.sharding import PartitionSpec as P

AXES = ("row", "col")
BF = jnp.bfloat16
F32 = jnp.float32
NT = (((1,), (1,)), ((), ()))


def linear(y, c, z, x):
    return (((y % 4) * 2 + c % 2) * 4 + z % 4) * 4 + x % 4


def pairs(move):
    return [
        (linear(y, c, z, x), linear(*move(y, c, z, x)))
        for y in range(4)
        for c in range(2)
        for z in range(4)
        for x in range(4)
    ]


def send(value, move):
    return lax.ppermute(value, AXES, pairs(move))


def shift_y(s):
    return lambda y, c, z, x: (y + s, c, z, x)


def swap_core(y, c, z, x):
    return (y, 1 - c, z, x)


def shift_first(s):
    return lambda y, c, z, x: (y, c, z + s * (1 - c), x + s * c)


def shift_second(s):
    return lambda y, c, z, x: (y, c, z + s * c, x + s * (1 - c))


def after(value, *others):
    return lax.optimization_barrier((value, *others))[0]


VMEM_SPEC = pl.BlockSpec(memory_space=pltpu.VMEM)
SMEM_SPEC = pl.BlockSpec(memory_space=pltpu.SMEM)
LIMIT = pltpu.CompilerParams(vmem_limit_bytes=16 * 1024 * 1024)


def in_vmem(value):
    return pltpu.with_memory_space_constraint(value, pltpu.VMEM)


def in_hbm(value):
    return pltpu.with_memory_space_constraint(value, pltpu.HBM)


def out_vmem(*shape):
    return pltpu.VMEM(shape, BF)


def cost(flops, moved):
    return pl.CostEstimate(flops=flops, transcendentals=0, bytes_accessed=moved)


def one_hot_eye():
    eye = (
        lax.broadcasted_iota(jnp.int32, (128, 128), 0)
        == lax.broadcasted_iota(jnp.int32, (128, 128), 1)
    )
    return jnp.where(eye, 1.0, 0.0).astype(BF)


def prepare_pairs(chol_pairs, order, part, held=()):
    block_b, block_d, aux = chol_pairs.shape

    def kernel(order_ref, in_ref, *refs):
        out_ref, columns = refs[len(held) :]

        @pl.when(pl.program_id(0) == 0)
        def _():
            q = lax.broadcasted_iota(jnp.int32, (aux, aux), 0)
            columns[...] = jnp.where(q == order_ref[...], 1.0, 0.0).astype(BF)

        target = lax.broadcasted_iota(jnp.int32, (256, 256), 0)
        source = lax.broadcasted_iota(jnp.int32, (256, 256), 1)
        rows = jnp.where((target % 16) * 16 + target // 16 == source, 1.0, 0.0).astype(BF)
        block = in_ref[...].reshape(256, aux)
        block = jnp.dot(rows, block, preferred_element_type=F32).astype(BF)
        block = jnp.dot(block, columns[...], preferred_element_type=F32).astype(BF)
        at = pl.ds(pl.multiple_of(pl.program_id(0) * 16, 16), 16)
        out_ref[:, at, :] = block.reshape(16, 16, aux)

    return pl.pallas_call(
        kernel,
        grid=(block_b // 16,),
        in_specs=[VMEM_SPEC, pl.BlockSpec((16, 16, aux), lambda i: (i, part, 0))]
        + [VMEM_SPEC] * len(held),
        out_specs=VMEM_SPEC,
        out_shape=out_vmem(16, block_b, aux),
        scratch_shapes=[pltpu.VMEM((aux, aux), BF)],
        cost_estimate=cost(block_b * block_d * aux * (aux + 256), 2 * block_b * block_d * aux),
        compiler_params=LIMIT,
        name="prepare_pairs",
    )(order, chol_pairs, *[in_vmem(h) for h in held])


def stack_up(pieces, cuts, held=()):
    rows, lanes = pieces[0].shape
    many = len(pieces)
    edges = [0, *cuts, lanes]
    spans = list(zip(edges[:-1], edges[1:]))

    def kernel(*refs):
        outs = refs[many + len(held) :]
        for n in range(many):
            for j, (start, stop) in enumerate(spans):
                outs[j][n] = refs[n][:, start:stop]

    return pl.pallas_call(
        kernel,
        in_specs=[VMEM_SPEC] * (many + len(held)),
        out_specs=[VMEM_SPEC] * len(spans),
        out_shape=[out_vmem(many, rows, stop - start) for start, stop in spans],
        compiler_params=LIMIT,
        name="stack_up",
    )(*[in_vmem(p) for p in [*pieces, *held]])


def turn_window(mine, theirs):
    depth, lanes = mine[0].shape[1:]
    aux = 32 * depth
    pieces = [*mine, *theirs]

    def kernel(*refs):
        out_ref = refs[8]
        eye = one_hot_eye()

        def columns(n, carry):
            at = pl.ds(pl.multiple_of(n * 128, 128), 128)
            for j in range(4):
                value = [refs[2 * j + m][:, :, at].reshape(4 * depth, 128) for m in range(2)]
                value = jnp.concatenate(value, axis=0)
                turned = lax.dot_general(eye, value, NT, preferred_element_type=F32)
                out_ref[at, 8 * depth * j : 8 * depth * (j + 1)] = turned.astype(BF)
            return carry

        lax.fori_loop(0, lanes // 128, columns, 0)

    return pl.pallas_call(
        kernel,
        in_specs=[VMEM_SPEC] * 8,
        out_specs=VMEM_SPEC,
        out_shape=out_vmem(lanes, aux),
        cost_estimate=cost(2 * lanes * aux * 256, 4 * lanes * aux),
        compiler_params=LIMIT,
        name="turn_window",
    )(*[in_vmem(p) for p in pieces])


def ladder_block(index, window, pairs_parts, amp_mine, amp_theirs, first):
    rows_c, aux = window.shape[1], window.shape[2]
    part_d, block_b, _ = pairs_parts[0].shape
    flats = [p.reshape(part_d * block_b, aux) for p in pairs_parts]
    depth = 2 * part_d * rows_c
    group = part_d // 2
    count = 16
    rows_o = amp_mine.shape[1]
    occ = 8 * rows_o

    def kernel(index_ref, window_ref, flat0, flat1, mine_ref, theirs_ref, o0, o1, o2, o3, w, ints):
        outs = (o0, o1, o2, o3)
        for n in range(count):
            w[n * rows_c : (n + 1) * rows_c, :] = window_ref[index_ref[first + n]]
        low = lax.broadcasted_iota(jnp.int32, (rows_c, 128), 1) < 64

        for g in range(4):
            at = slice((g % 2) * group * block_b, (g % 2 + 1) * group * block_b)
            right = (flat0, flat1)[g // 2][at, :]
            value = lax.dot_general(w[...], right, NT, preferred_element_type=F32)
            for p in range(count // 2):
                for t in range(group // 2):
                    u = value[2 * p * rows_c : (2 * p + 1) * rows_c, 128 * t : 128 * (t + 1)]
                    v = value[(2 * p + 1) * rows_c : (2 * p + 2) * rows_c, 128 * t : 128 * (t + 1)]
                    one = jnp.where(low, u, pltpu.roll(v, 64, 1)).astype(BF)
                    two = jnp.where(low, pltpu.roll(u, 64, 1), v).astype(BF)
                    base = (g * group + 2 * t) * rows_c
                    ints[base : base + rows_c, 128 * p : 128 * (p + 1)] = one
                    ints[base + rows_c : base + 2 * rows_c, 128 * p : 128 * (p + 1)] = two

        for n in range(4):
            right = ints[:, 256 * n : 256 * (n + 1)]
            for k, ref in enumerate((mine_ref, theirs_ref)):
                left = ref[...].reshape(4 * rows_o, depth)
                value = jnp.dot(left, right, preferred_element_type=F32).astype(BF)
                for m in range(4):
                    rows = pl.ds(pl.multiple_of(index_ref[4 * k + m] * rows_o, rows_o), rows_o)
                    outs[n][rows, :] = value[m * rows_o : (m + 1) * rows_o]

    return pl.pallas_call(
        kernel,
        in_specs=[SMEM_SPEC] + [VMEM_SPEC] * 5,
        out_specs=[VMEM_SPEC] * 4,
        scratch_shapes=[
            pltpu.VMEM((count * rows_c, aux), BF),
            pltpu.VMEM((depth, count * block_b), BF),
        ],
        out_shape=[out_vmem(occ, 4 * block_b)] * 4,
        cost_estimate=cost(2 * count * rows_c * depth * block_b * (aux + occ) // rows_c, 2000000),
        compiler_params=LIMIT,
        name="ladder_block",
    )(index, in_vmem(window), *[in_vmem(f) for f in flats], in_vmem(amp_mine), in_vmem(amp_theirs))


def add_and_turn(groups):
    occ, lanes = groups[0][0].shape
    many = len(groups)

    def kernel(*refs):
        outs = refs[4 * many :]
        eye = one_hot_eye()
        for j in range(many):
            p = refs[4 * j : 4 * j + 4]
            total = (p[0][...].astype(F32) + p[1][...].astype(F32)) + (
                p[2][...].astype(F32) + p[3][...].astype(F32)
            )
            total = total.astype(BF)
            for n in range(lanes // 128):
                turned = lax.dot_general(
                    eye, total[:, n * 128 : (n + 1) * 128], NT, preferred_element_type=F32
                ).astype(BF)
                for h in range(2):
                    outs[2 * n + h][64 * j : 64 * j + 64, :] = turned[h * 64 : h * 64 + 64]

    return pl.pallas_call(
        kernel,
        in_specs=[VMEM_SPEC] * (4 * many),
        out_specs=[VMEM_SPEC] * 4,
        out_shape=[out_vmem(64 * many, occ)] * 4,
        cost_estimate=cost(2 * occ * lanes * 256, 3000000),
        compiler_params=LIMIT,
        name="add_and_turn",
    )(*[in_vmem(p) for group in groups for p in group])


def dress(index, pieces, eps_pair, eps_occupied, dress_first, dress_second):
    rows, occ = eps_pair.shape[0], eps_occupied.shape[1]
    rows_b = 64
    rows_a = rows // rows_b
    heights = [group[0].shape[0] for group in pieces]

    def kernel(index_ref, *refs):
        ins, refs = refs[: 4 * len(pieces)], refs[4 * len(pieces) :]
        pair_ref, occ_ref, first_ref, second_ref = refs[:4]
        outs, (ladder, mixed, right, sem) = refs[4:6], refs[6:]
        copies = [
            pltpu.make_async_copy(ref, right.at[n], sem.at[n])
            for n, ref in enumerate((first_ref, second_ref))
        ]
        for copy in copies:
            copy.start()
        base = 0
        for n, height in enumerate(heights):
            p = [ref[...].astype(F32) for ref in ins[4 * n : 4 * n + 4]]
            ladder[base : base + height, :] = (p[0] + p[1]) + (p[2] + p[3])
            base += height
        scaled = (ladder[...] / (pair_ref[...] + occ_ref[...])).astype(BF)
        copies[0].wait()
        first = jnp.dot(scaled, right[0], preferred_element_type=F32).astype(BF)
        copies[1].wait()
        second = jnp.dot(first, right[1], preferred_element_type=F32)
        mixed[...] = scaled.astype(F32) + second
        for n in range(8):
            at = pl.ds(pl.multiple_of(index_ref[8 + n] * 128, 128), 128)
            outs[n // 4][n % 4] = mixed[:, at].astype(BF).reshape(rows_a, rows_b, 128)

    flat = [in_vmem(p) for group in pieces for p in group]
    return pl.pallas_call(
        kernel,
        in_specs=[SMEM_SPEC]
        + [VMEM_SPEC] * (len(flat) + 2)
        + [pl.BlockSpec(memory_space=pltpu.HBM)] * 2,
        out_specs=[VMEM_SPEC] * 2,
        out_shape=[out_vmem(4, rows_a, rows_b, 128)] * 2,
        scratch_shapes=[
            pltpu.VMEM((rows, occ), F32),
            pltpu.VMEM((rows, occ), F32),
            pltpu.VMEM((2, occ, occ), BF),
            pltpu.SemaphoreType.DMA((2,)),
        ],
        cost_estimate=cost(4 * rows * occ * occ, 6000000),
        compiler_params=LIMIT,
        name="dress",
    )(index, *flat, eps_pair, eps_occupied, in_hbm(dress_first), in_hbm(dress_second))


def pair_up(mine, theirs):
    shape = mine.shape

    def kernel(mine_ref, theirs_ref, *outs):
        for n in range(4):
            outs[n][0] = mine_ref[n]
            outs[n][1] = theirs_ref[n]

    return pl.pallas_call(
        kernel,
        in_specs=[VMEM_SPEC] * 2,
        out_specs=[VMEM_SPEC] * 4,
        out_shape=[out_vmem(2, *shape[1:])] * 4,
        compiler_params=LIMIT,
        name="pair_up",
    )(in_vmem(mine), in_vmem(theirs))


def place(index, blocks):
    _, rows_a, rows_b, lanes = blocks[0].shape

    def kernel(index_ref, *refs):
        for n in range(8):
            at = pl.ds(pl.multiple_of(index_ref[n] * rows_b, rows_b), rows_b)
            refs[4][:, at, :] = refs[n % 4][n // 4]

    return pl.pallas_call(
        kernel,
        in_specs=[SMEM_SPEC] + [VMEM_SPEC] * 4,
        out_specs=VMEM_SPEC,
        out_shape=jax.ShapeDtypeStruct((rows_a, 8 * rows_b, lanes), BF),
        compiler_params=LIMIT,
        name="place",
    )(index, *[in_vmem(p) for p in blocks])


def local(
    chol_window,
    chol_pairs,
    amplitudes,
    eps_window,
    eps_virtual,
    eps_occupied,
    dress_first,
    dress_second,
):
    row, col = lax.axis_index("row"), lax.axis_index("col")
    y, core, z, x = row // 2, row % 2, col // 4, col % 4
    window_size, own_aux = chol_window.shape[0], chol_window.shape[2]
    block_b, block_d, aux = chol_pairs.shape
    occ_block = amplitudes.shape[2]
    rows_a = window_size // 16
    part = 16 * window_size
    shifts = (1, 2, 3)

    own = jnp.transpose(chol_window.reshape(16, rows_a, window_size, own_aux), (3, 1, 0, 2))
    own = own.reshape(own_aux, rows_a * part)
    sent = []
    for s in shifts:
        sent.append(send(own, shift_y(s)))

    k = jnp.arange(aux, dtype=jnp.int32)
    i, slot = k % own_aux, k // own_aux
    s_y, v, u, c = slot % 4, (slot // 4) % 4, (slot // 16) % 4, (core + slot // 64) % 2
    k_z = jnp.where(c == 0, z - v, z - u) % 4
    k_x = jnp.where(c == 0, x - u, x - v) % 4
    order = (((((y - s_y) % 4) * 2 + c) * 4 + k_z) * 4 + k_x) * own_aux + i
    order = order.astype(jnp.int32)[None, :]
    amp = jnp.transpose(amplitudes, (2, 1, 0)).reshape(occ_block, block_d * window_size)

    n = jnp.arange(16, dtype=jnp.int32)
    s = jnp.arange(4, dtype=jnp.int32)
    owner = jnp.where(
        core == 0,
        4 * ((z + n // 4) % 4) + (x + n % 4) % 4,
        4 * ((z + n % 4) % 4) + (x + n // 4) % 4,
    )
    index = [((y - s) % 4) * 2 + core, ((y - s) % 4) * 2 + 1 - core]
    index += [((y + s) % 4) * 2 + core, ((y + s) % 4) * 2 + 1 - core]
    index += [owner, owner, owner + 16]
    index = jnp.concatenate(index).astype(jnp.int32)
    eps_pair = (eps_window[:, None] + eps_virtual[None, :]).reshape(rows_a * block_b, 1)
    amp_sent = []
    for m in shifts:
        amp_sent.append(send(amp, shift_y(m)))
    sent[0], index, eps_pair, order = lax.optimization_barrier(
        (sent[0], index, eps_pair, order)
    )

    both = jnp.concatenate([own] + sent, axis=0)
    plane = [send(both, shift_first(s)) for s in shifts]

    chol_pairs = in_hbm(chol_pairs)
    pairs_one = prepare_pairs(chol_pairs, after(order, both), 0)
    *plane, pairs_one = lax.optimization_barrier((*plane, pairs_one))
    plane = [both] + plane

    groups = []
    for piece in stack_up(plane, (part,), (pairs_one,)):
        group = [piece]
        for s in shifts:
            group.append(send(piece, shift_second(s)))
        groups.append(group)
    swapped = [send(group[0], swap_core) for group in groups]
    amp_mine = jnp.stack([amp] + amp_sent)
    amp_theirs = send(amp_mine, swap_core)
    pairs_two = prepare_pairs(
        chol_pairs, after(order, groups[1][0], pairs_one, amp_mine), 1, (pairs_one,)
    )
    *groups[0], pairs_two = lax.optimization_barrier((*groups[0], pairs_two))

    def turn(group, first):
        theirs = [first]
        for p in group[1:]:
            theirs.append(send(p, swap_core))
        turned = turn_window(group, theirs)
        return turned.reshape(turned.shape[0] // window_size, window_size, aux)

    window = turn(groups[0], swapped[0])

    parts, sums = [], []
    for a in range(rows_a):
        if a == 1:
            groups[1] = lax.optimization_barrier((*groups[1], *parts[0]))[:4]
            window = turn(groups[1], swapped[1])
        if a == 2:
            window = after(window, *parts[1])
        outs = ladder_block(
            index, window, (pairs_one, pairs_two), amp_mine, amp_theirs, 16 + 16 * a
        )
        parts.append(outs)
        received = [outs[0]]
        for m in (2, 1, 3):
            received.append(send(outs[m], shift_first(m)))
        sums.append(received)
    mine = add_and_turn(sums)
    pieces = [[mine[0]] + [send(mine[m], shift_second(m)) for m in (2, 1, 3)]]

    mine, give = dress(index, pieces, eps_pair, eps_occupied[None, :], dress_first, dress_second)
    blocks = pair_up(mine, send(give, swap_core))
    blocks = [blocks[0]] + [send(blocks[s], shift_y(s)) for s in shifts]
    return place(index, blocks)


def solution(mesh):
    return jax.shard_map(
        local,
        mesh=mesh,
        in_specs=(
            P(None, None, ("row", "col")),
            P("row", "col", None),
            P(None, "col", "row"),
            P("col"),
            P("row"),
            P(),
            P(),
            P(),
        ),
        out_specs=P("col", None, "row"),
        check_vma=False,
    )
```

```python
import jax
import jax.numpy as jnp
from jax import lax
from jax.experimental import pallas as pl
from jax.experimental.pallas import tpu as pltpu
from jax.sharding import PartitionSpec as P

AXES = ("row", "col")
BF = jnp.bfloat16
F32 = jnp.float32
NT = (((1,), (1,)), ((), ()))


def linear(y, c, z, x):
    return (((y % 4) * 2 + c % 2) * 4 + z % 4) * 4 + x % 4


def pairs(move):
    return [
        (linear(y, c, z, x), linear(*move(y, c, z, x)))
        for y in range(4)
        for c in range(2)
        for z in range(4)
        for x in range(4)
    ]


def send(value, move):
    return lax.ppermute(value, AXES, pairs(move))


def shift_y(s):
    return lambda y, c, z, x: (y + s, c, z, x)


def swap_core(y, c, z, x):
    return (y, 1 - c, z, x)


def shift_first(s):
    return lambda y, c, z, x: (y, c, z + s * (1 - c), x + s * c)


def shift_second(s):
    return lambda y, c, z, x: (y, c, z + s * c, x + s * (1 - c))


def after(value, *others):
    return lax.optimization_barrier((value, *others))[0]


VMEM_SPEC = pl.BlockSpec(memory_space=pltpu.VMEM)
SMEM_SPEC = pl.BlockSpec(memory_space=pltpu.SMEM)
LOOPED = (0,)
LIMIT = pltpu.CompilerParams(vmem_limit_bytes=16 * 1024 * 1024)


def in_vmem(value):
    return pltpu.with_memory_space_constraint(value, pltpu.VMEM)


def in_hbm(value):
    return pltpu.with_memory_space_constraint(value, pltpu.HBM)


def out_vmem(*shape):
    return pltpu.VMEM(shape, BF)


def cost(flops, moved):
    return pl.CostEstimate(flops=flops, transcendentals=0, bytes_accessed=moved)


def one_hot_eye():
    eye = (
        lax.broadcasted_iota(jnp.int32, (128, 128), 0)
        == lax.broadcasted_iota(jnp.int32, (128, 128), 1)
    )
    return jnp.where(eye, 1.0, 0.0).astype(BF)


def prepare_pairs(chol_pairs, order, part, held=()):
    block_b, block_d, aux = chol_pairs.shape

    def kernel(order_ref, in_ref, *refs):
        out_ref, columns = refs[len(held) :]

        @pl.when(pl.program_id(0) == 0)
        def _():
            q = lax.broadcasted_iota(jnp.int32, (aux, aux), 0)
            columns[...] = jnp.where(q == order_ref[...], 1.0, 0.0).astype(BF)

        target = lax.broadcasted_iota(jnp.int32, (256, 256), 0)
        source = lax.broadcasted_iota(jnp.int32, (256, 256), 1)
        rows = jnp.where((target % 16) * 16 + target // 16 == source, 1.0, 0.0).astype(BF)
        block = in_ref[...].reshape(256, aux)
        block = jnp.dot(rows, block, preferred_element_type=F32).astype(BF)
        block = jnp.dot(block, columns[...], preferred_element_type=F32).astype(BF)
        at = pl.ds(pl.multiple_of(pl.program_id(0) * 16, 16), 16)
        out_ref[:, at, :] = block.reshape(16, 16, aux)

    return pl.pallas_call(
        kernel,
        grid=(block_b // 16,),
        in_specs=[VMEM_SPEC, pl.BlockSpec((16, 16, aux), lambda i: (i, part, 0))]
        + [VMEM_SPEC] * len(held),
        out_specs=VMEM_SPEC,
        out_shape=out_vmem(16, block_b, aux),
        scratch_shapes=[pltpu.VMEM((aux, aux), BF)],
        cost_estimate=cost(block_b * block_d * aux * (aux + 256), 2 * block_b * block_d * aux),
        compiler_params=LIMIT,
        name="prepare_pairs",
    )(order, chol_pairs, *[in_vmem(h) for h in held])


def stack_up(pieces, cuts, held=()):
    rows, lanes = pieces[0].shape
    many = len(pieces)
    edges = [0, *cuts, lanes]
    spans = list(zip(edges[:-1], edges[1:]))

    def kernel(*refs):
        outs = refs[many + len(held) :]
        for n in range(many):
            for j, (start, stop) in enumerate(spans):
                outs[j][n] = refs[n][:, start:stop]

    return pl.pallas_call(
        kernel,
        in_specs=[VMEM_SPEC] * (many + len(held)),
        out_specs=[VMEM_SPEC] * len(spans),
        out_shape=[out_vmem(many, rows, stop - start) for start, stop in spans],
        compiler_params=LIMIT,
        name="stack_up",
    )(*[in_vmem(p) for p in [*pieces, *held]])


def turn_window(mine, theirs):
    depth, lanes = mine[0].shape[1:]
    aux = 32 * depth
    pieces = [*mine, *theirs]

    def kernel(*refs):
        out_ref = refs[8]
        eye = one_hot_eye()

        def columns(n, carry):
            at = pl.ds(pl.multiple_of(n * 128, 128), 128)
            for j in range(4):
                value = [refs[2 * j + m][:, :, at].reshape(4 * depth, 128) for m in range(2)]
                value = jnp.concatenate(value, axis=0)
                turned = lax.dot_general(eye, value, NT, preferred_element_type=F32)
                out_ref[at, 8 * depth * j : 8 * depth * (j + 1)] = turned.astype(BF)
            return carry

        lax.fori_loop(0, lanes // 128, columns, 0)

    return pl.pallas_call(
        kernel,
        in_specs=[VMEM_SPEC] * 8,
        out_specs=VMEM_SPEC,
        out_shape=out_vmem(lanes, aux),
        cost_estimate=cost(2 * lanes * aux * 256, 4 * lanes * aux),
        compiler_params=LIMIT,
        name="turn_window",
    )(*[in_vmem(p) for p in pieces])


def ladder_block(index, window, pairs_parts, amp_mine, amp_theirs, first, loop):
    rows_c, aux = window.shape[1], window.shape[2]
    part_d, block_b, _ = pairs_parts[0].shape
    flats = [p.reshape(part_d * block_b, aux) for p in pairs_parts]
    depth = 2 * part_d * rows_c
    group = part_d // 2
    count = 16
    rows_o = amp_mine.shape[1]
    occ = 8 * rows_o

    def kernel(index_ref, window_ref, flat0, flat1, mine_ref, theirs_ref, o0, o1, o2, o3, w, ints, out):
        outs = (o0, o1, o2, o3)
        for n in range(count):
            w[n * rows_c : (n + 1) * rows_c, :] = window_ref[index_ref[first + n]]
        low = lax.broadcasted_iota(jnp.int32, (rows_c, 128), 1) < 64

        for g in range(4):
            at = slice((g % 2) * group * block_b, (g % 2 + 1) * group * block_b)
            right = (flat0, flat1)[g // 2][at, :]
            value = lax.dot_general(w[...], right, NT, preferred_element_type=F32)
            for p in range(count // 2):
                for t in range(group // 2):
                    u = value[2 * p * rows_c : (2 * p + 1) * rows_c, 128 * t : 128 * (t + 1)]
                    v = value[(2 * p + 1) * rows_c : (2 * p + 2) * rows_c, 128 * t : 128 * (t + 1)]
                    one = jnp.where(low, u, pltpu.roll(v, 64, 1)).astype(BF)
                    two = jnp.where(low, pltpu.roll(u, 64, 1), v).astype(BF)
                    base = (g * group + 2 * t) * rows_c
                    ints[base : base + rows_c, 128 * p : 128 * (p + 1)] = one
                    ints[base + rows_c : base + 2 * rows_c, 128 * p : 128 * (p + 1)] = two

        def product(n, write):
            right = ints[:, pl.ds(pl.multiple_of(n * 256, 256), 256)]
            for k, ref in enumerate((mine_ref, theirs_ref)):
                left = ref[...].reshape(4 * rows_o, depth)
                value = jnp.dot(left, right, preferred_element_type=F32).astype(BF)
                for m in range(4):
                    rows = pl.ds(pl.multiple_of(index_ref[4 * k + m] * rows_o, rows_o), rows_o)
                    write[rows, :] = value[m * rows_o : (m + 1) * rows_o]

        def looped(n, carry):
            product(n, out)
            for j in range(4):

                @pl.when(n == j)
                def _():
                    outs[j][...] = out[...]

            return carry

        if loop:
            lax.fori_loop(0, 4, looped, 0)
        else:
            for n in range(4):
                product(n, outs[n])

    return pl.pallas_call(
        kernel,
        in_specs=[SMEM_SPEC] + [VMEM_SPEC] * 5,
        out_specs=[VMEM_SPEC] * 4,
        scratch_shapes=[
            pltpu.VMEM((count * rows_c, aux), BF),
            pltpu.VMEM((depth, count * block_b), BF),
            pltpu.VMEM((occ, 4 * block_b), BF),
        ],
        out_shape=[out_vmem(occ, 4 * block_b)] * 4,
        cost_estimate=cost(2 * count * rows_c * depth * block_b * (aux + occ) // rows_c, 2000000),
        compiler_params=LIMIT,
        name="ladder_block",
    )(index, in_vmem(window), *[in_vmem(f) for f in flats], in_vmem(amp_mine), in_vmem(amp_theirs))


def add_and_turn(groups):
    occ, lanes = groups[0][0].shape
    many = len(groups)

    def kernel(*refs):
        outs = refs[4 * many :]
        eye = one_hot_eye()
        for j in range(many):
            p = refs[4 * j : 4 * j + 4]
            total = (p[0][...].astype(F32) + p[1][...].astype(F32)) + (
                p[2][...].astype(F32) + p[3][...].astype(F32)
            )
            total = total.astype(BF)
            for n in range(lanes // 128):
                turned = lax.dot_general(
                    eye, total[:, n * 128 : (n + 1) * 128], NT, preferred_element_type=F32
                ).astype(BF)
                for h in range(2):
                    outs[2 * n + h][64 * j : 64 * j + 64, :] = turned[h * 64 : h * 64 + 64]

    return pl.pallas_call(
        kernel,
        in_specs=[VMEM_SPEC] * (4 * many),
        out_specs=[VMEM_SPEC] * 4,
        out_shape=[out_vmem(64 * many, occ)] * 4,
        cost_estimate=cost(2 * occ * lanes * 256, 3000000),
        compiler_params=LIMIT,
        name="add_and_turn",
    )(*[in_vmem(p) for group in groups for p in group])


def dress(index, pieces, eps_pair, eps_occupied, dress_first, dress_second):
    rows, occ = eps_pair.shape[0], eps_occupied.shape[1]
    rows_b = 64
    rows_a = rows // rows_b
    heights = [group[0].shape[0] for group in pieces]

    def kernel(index_ref, *refs):
        ins, refs = refs[: 4 * len(pieces)], refs[4 * len(pieces) :]
        pair_ref, occ_ref, first_ref, second_ref = refs[:4]
        outs, (ladder, mixed, right, sem) = refs[4:6], refs[6:]
        copies = [
            pltpu.make_async_copy(ref, right.at[n], sem.at[n])
            for n, ref in enumerate((first_ref, second_ref))
        ]
        for copy in copies:
            copy.start()
        base = 0
        for n, height in enumerate(heights):
            p = [ref[...].astype(F32) for ref in ins[4 * n : 4 * n + 4]]
            ladder[base : base + height, :] = (p[0] + p[1]) + (p[2] + p[3])
            base += height
        scaled = (ladder[...] / (pair_ref[...] + occ_ref[...])).astype(BF)
        copies[0].wait()
        first = jnp.dot(scaled, right[0], preferred_element_type=F32).astype(BF)
        copies[1].wait()
        second = jnp.dot(first, right[1], preferred_element_type=F32)
        mixed[...] = scaled.astype(F32) + second
        for n in range(8):
            at = pl.ds(pl.multiple_of(index_ref[8 + n] * 128, 128), 128)
            outs[n // 4][n % 4] = mixed[:, at].astype(BF).reshape(rows_a, rows_b, 128)

    flat = [in_vmem(p) for group in pieces for p in group]
    return pl.pallas_call(
        kernel,
        in_specs=[SMEM_SPEC]
        + [VMEM_SPEC] * (len(flat) + 2)
        + [pl.BlockSpec(memory_space=pltpu.HBM)] * 2,
        out_specs=[VMEM_SPEC] * 2,
        out_shape=[out_vmem(4, rows_a, rows_b, 128)] * 2,
        scratch_shapes=[
            pltpu.VMEM((rows, occ), F32),
            pltpu.VMEM((rows, occ), F32),
            pltpu.VMEM((2, occ, occ), BF),
            pltpu.SemaphoreType.DMA((2,)),
        ],
        cost_estimate=cost(4 * rows * occ * occ, 6000000),
        compiler_params=LIMIT,
        name="dress",
    )(index, *flat, eps_pair, eps_occupied, in_hbm(dress_first), in_hbm(dress_second))


def pair_up(mine, theirs):
    shape = mine.shape

    def kernel(mine_ref, theirs_ref, *outs):
        for n in range(4):
            outs[n][0] = mine_ref[n]
            outs[n][1] = theirs_ref[n]

    return pl.pallas_call(
        kernel,
        in_specs=[VMEM_SPEC] * 2,
        out_specs=[VMEM_SPEC] * 4,
        out_shape=[out_vmem(2, *shape[1:])] * 4,
        compiler_params=LIMIT,
        name="pair_up",
    )(in_vmem(mine), in_vmem(theirs))


def place(index, blocks):
    _, rows_a, rows_b, lanes = blocks[0].shape

    def kernel(index_ref, *refs):
        for n in range(8):
            at = pl.ds(pl.multiple_of(index_ref[n] * rows_b, rows_b), rows_b)
            refs[4][:, at, :] = refs[n % 4][n // 4]

    return pl.pallas_call(
        kernel,
        in_specs=[SMEM_SPEC] + [VMEM_SPEC] * 4,
        out_specs=VMEM_SPEC,
        out_shape=jax.ShapeDtypeStruct((rows_a, 8 * rows_b, lanes), BF),
        compiler_params=LIMIT,
        name="place",
    )(index, *[in_vmem(p) for p in blocks])


def local(
    chol_window,
    chol_pairs,
    amplitudes,
    eps_window,
    eps_virtual,
    eps_occupied,
    dress_first,
    dress_second,
):
    row, col = lax.axis_index("row"), lax.axis_index("col")
    y, core, z, x = row // 2, row % 2, col // 4, col % 4
    window_size, own_aux = chol_window.shape[0], chol_window.shape[2]
    block_b, block_d, aux = chol_pairs.shape
    occ_block = amplitudes.shape[2]
    rows_a = window_size // 16
    part = 16 * window_size
    shifts = (1, 2, 3)

    own = jnp.transpose(chol_window.reshape(16, rows_a, window_size, own_aux), (3, 1, 0, 2))
    own = own.reshape(own_aux, rows_a * part)
    sent = []
    for s in shifts:
        sent.append(send(own, shift_y(s)))

    k = jnp.arange(aux, dtype=jnp.int32)
    i, slot = k % own_aux, k // own_aux
    s_y, v, u, c = slot % 4, (slot // 4) % 4, (slot // 16) % 4, (core + slot // 64) % 2
    k_z = jnp.where(c == 0, z - v, z - u) % 4
    k_x = jnp.where(c == 0, x - u, x - v) % 4
    order = (((((y - s_y) % 4) * 2 + c) * 4 + k_z) * 4 + k_x) * own_aux + i
    order = order.astype(jnp.int32)[None, :]
    amp = jnp.transpose(amplitudes, (2, 1, 0)).reshape(occ_block, block_d * window_size)

    n = jnp.arange(16, dtype=jnp.int32)
    s = jnp.arange(4, dtype=jnp.int32)
    owner = jnp.where(
        core == 0,
        4 * ((z + n // 4) % 4) + (x + n % 4) % 4,
        4 * ((z + n % 4) % 4) + (x + n // 4) % 4,
    )
    index = [((y - s) % 4) * 2 + core, ((y - s) % 4) * 2 + 1 - core]
    index += [((y + s) % 4) * 2 + core, ((y + s) % 4) * 2 + 1 - core]
    index += [owner, owner, owner + 16]
    index = jnp.concatenate(index).astype(jnp.int32)
    eps_pair = (eps_window[:, None] + eps_virtual[None, :]).reshape(rows_a * block_b, 1)
    amp_sent = []
    for m in shifts:
        amp_sent.append(send(amp, shift_y(m)))
    sent[0], index, eps_pair, order = lax.optimization_barrier(
        (sent[0], index, eps_pair, order)
    )

    both = jnp.concatenate([own] + sent, axis=0)
    plane = [send(both, shift_first(s)) for s in shifts]

    chol_pairs = in_hbm(chol_pairs)
    pairs_one = prepare_pairs(chol_pairs, after(order, both), 0)
    *plane, pairs_one = lax.optimization_barrier((*plane, pairs_one))
    plane = [both] + plane

    groups = []
    for piece in stack_up(plane, (part,), (pairs_one,)):
        group = [piece]
        for s in shifts:
            group.append(send(piece, shift_second(s)))
        groups.append(group)
    swapped = [send(group[0], swap_core) for group in groups]
    amp_mine = jnp.stack([amp] + amp_sent)
    amp_theirs = send(amp_mine, swap_core)
    pairs_two = prepare_pairs(
        chol_pairs, after(order, groups[1][0], pairs_one, amp_mine), 1, (pairs_one,)
    )
    *groups[0], pairs_two = lax.optimization_barrier((*groups[0], pairs_two))

    def turn(group, first):
        theirs = [first]
        for p in group[1:]:
            theirs.append(send(p, swap_core))
        turned = turn_window(group, theirs)
        return turned.reshape(turned.shape[0] // window_size, window_size, aux)

    window = turn(groups[0], swapped[0])

    parts, sums = [], []
    for a in range(rows_a):
        if a == 1:
            groups[1] = lax.optimization_barrier((*groups[1], *parts[0]))[:4]
            window = turn(groups[1], swapped[1])
        if a == 2:
            window = after(window, *parts[1])
        outs = ladder_block(
            index, window, (pairs_one, pairs_two), amp_mine, amp_theirs, 16 + 16 * a, a in LOOPED
        )
        parts.append(outs)
        received = [outs[0]]
        for m in (2, 1, 3):
            received.append(send(outs[m], shift_first(m)))
        sums.append(received)
    mine = add_and_turn(sums)
    pieces = [[mine[0]] + [send(mine[m], shift_second(m)) for m in (2, 1, 3)]]

    mine, give = dress(index, pieces, eps_pair, eps_occupied[None, :], dress_first, dress_second)
    blocks = pair_up(mine, send(give, swap_core))
    blocks = [blocks[0]] + [send(blocks[s], shift_y(s)) for s in shifts]
    return place(index, blocks)


def solution(mesh):
    return jax.shard_map(
        local,
        mesh=mesh,
        in_specs=(
            P(None, None, ("row", "col")),
            P("row", "col", None),
            P(None, "col", "row"),
            P("col"),
            P("row"),
            P(),
            P(),
            P(),
        ),
        out_specs=P("col", None, "row"),
        check_vma=False,
    )
```
